32 devices in a mesh: dp: 4 (over y, core), blk: 8 (over z, x).
Axes of the slice: x: 2, y: 2, z: 4, core: 2. Of those that a mesh axis runs over, the one named last changes fastest.
Arguments:
- pre_gelu: bfloat16 [6144, 4096], P(('dp', 'blk')), may hold values from -8 to 8
- out_grad: bfloat16 [6144, 1024], P(('dp', 'blk')), may hold values from -6 to 6
- down_weight: bfloat16 [4096, 1024], P('blk'), may hold values from -0.09375 to 0.09375
Outputs:
- block_out: bfloat16 [6144, 1024], P(('dp', 'blk'))
- pre_grad: bfloat16 [6144, 4096], P(('dp', 'blk'))
- weight_grad: float32 [4096, 1024], P('blk')
The draws below stay inside these ranges and needn't reach their ends.
All inputs are finite; a program needn't handle non-finite values.
Results may differ from the reference program's by a relative error of at most 0.017.
Values may be sent and summed in bfloat16 or wider, within the bound.
No kernel may reach another device: no remote copies, remote signals or barrier semaphores. Data moves between devices by JAX's collectives and lax.ppermute only.
A program may use at most 64 MiB of HBM per device.

```python
import math
import jax
import jax.numpy as jnp
from jax import lax

D = 1024
FF = 4096
ROWS_DEV = 192
TOKENS = 6144
N_DP = 4
N_BLK = 8


def steps_of(own_key, dims, shards, least, largest):
    def one(position, shards_of):
        draws = jax.random.uniform(jax.random.fold_in(jax.random.fold_in(own_key, 6), position), (shards_of,), jnp.float32, least / len(shards), largest / len(shards))
        return jnp.repeat(jnp.exp(draws), dims[position] // shards_of).reshape((-1,) + (1,) * (len(dims) - position - 1))

    loudness = one(*shards[0])
    for cut in shards[1:]:
        loudness = loudness * one(*cut)
    return loudness


def bell_draw(stream_key, extent, scale, limit, cuts=(), kind=jnp.bfloat16):
    values = scale * jax.random.normal(stream_key, extent, jnp.float32)
    if cuts:
        values = values * steps_of(stream_key, extent, cuts, -0.22, 0.18)
    return jnp.clip(values, -limit, limit).astype(kind)


def setup_inputs(seed: int = 0) -> dict:
    streams_of = jax.random.split(jax.random.key(seed), 4)
    return {
        "pre_gelu": bell_draw(streams_of[0], (TOKENS, FF), 1.5, 8.0, ((0, 32),)),
        "out_grad": bell_draw(streams_of[1], (TOKENS, D), 1.0, 6.0, ((0, 32),)),
        "down_weight": bell_draw(streams_of[2], (FF, D), FF ** -0.5, 0.09375, ((0, 8),)),
    }


SQRT_TWO_PI = 0.7978845608028654
CUBIC = 0.044715

def gelu_parts(inputs):
    argument = SQRT_TWO_PI * (inputs + CUBIC * inputs * inputs * inputs)
    tangent = jnp.tanh(argument)
    activation = 0.5 * inputs * (1.0 + tangent)
    derivative = 0.5 * (1.0 + tangent) + 0.5 * inputs * (1.0 - tangent * tangent) * SQRT_TWO_PI * (1.0 + 3.0 * CUBIC * inputs * inputs)
    return (activation, derivative)

def group_pass(pre_group, grad_group, down_weight):
    activation, derivative = gelu_parts(pre_group.astype(jnp.float32))
    hidden = activation.astype(jnp.bfloat16)
    output = jnp.dot(hidden, down_weight, preferred_element_type=jnp.float32).astype(jnp.bfloat16)
    d_hidden = jnp.dot(grad_group, down_weight.T, preferred_element_type=jnp.float32)
    pre_grad = (d_hidden * derivative).astype(jnp.bfloat16)
    blocks = FF // N_BLK
    stacked = hidden.reshape(N_BLK, ROWS_DEV, N_BLK, blocks)
    targets = grad_group.reshape(N_BLK, ROWS_DEV, D)
    diagonal = jnp.arange(N_BLK)

    def add_stop(accumulated, offset):
        shifted = jnp.roll(stacked, -offset, axis=0)[diagonal, :, diagonal, :]
        paired = jnp.roll(targets, -offset, axis=0)
        contribution = jnp.einsum('brf,brd->bfd', shifted.astype(jnp.float32), paired.astype(jnp.float32))
        return ((accumulated.astype(jnp.float32) + contribution).astype(jnp.bfloat16), offset)
    initial = jnp.zeros((N_BLK, blocks, D), jnp.bfloat16)
    accumulated = lax.scan(add_stop, initial, jnp.arange(1, N_BLK + 1, dtype=jnp.int32))[0]
    return (output, pre_grad, accumulated.reshape(FF, D))

def reference(pre_gelu, out_grad, down_weight):
    groups_pre = pre_gelu.reshape(N_DP, N_BLK * ROWS_DEV, FF)
    groups_grad = out_grad.reshape(N_DP, N_BLK * ROWS_DEV, D)

    def per_group(summed, pieces):
        output, pre_grad, accumulated = group_pass(pieces[0], pieces[1], down_weight)
        return (summed + accumulated.astype(jnp.float32), (output, pre_grad))
    summed, results = lax.scan(per_group, jnp.zeros((FF, D), jnp.float32), (groups_pre, groups_grad))
    weight_grad = summed / math.sqrt(TOKENS)
    return (results[0].reshape(TOKENS, D), results[1].reshape(TOKENS, FF), weight_grad)
```

```python
import functools
import math

import jax
import jax.numpy as jnp
from jax import lax
from jax.experimental import pallas as pl
from jax.experimental.pallas import tpu as pltpu
from jax.sharding import PartitionSpec as P

SQRT_TWO_PI = 0.7978845608028654
CUBIC = 0.044715
AXES = ("dp", "blk")
VMEM_LIMIT = 48 * 1024 * 1024


def gelu_parts(inputs):
    square = inputs * inputs
    tangent = jnp.tanh(SQRT_TWO_PI * (inputs + CUBIC * (square * inputs)))
    half = 0.5 * (1.0 + tangent)
    activation = inputs * half
    derivative = half + 0.5 * inputs * (1.0 - tangent * tangent) * (
        SQRT_TWO_PI * (1.0 + 3.0 * CUBIC * square)
    )
    return activation, derivative


def gelu(inputs):
    square = inputs * inputs
    tangent = jnp.tanh(SQRT_TWO_PI * (inputs + CUBIC * (square * inputs)))
    return inputs * (0.5 * (1.0 + tangent))


def dot(a, b, contract):
    return lax.dot_general(a, b, ((contract[0:1], contract[1:2]), ((), ())), preferred_element_type=jnp.float32)


def piece_at(info, core, row, cores, rows):
    return lax.rem(info[0] + core, cores) * rows + lax.rem(info[1] + row, rows)


def weight_terms(cores, rows, info, ids, pre_own, pre_other, grad_own, grad_other, keep, send, total):
    own = gelu(pre_own[...].astype(jnp.float32)).astype(jnp.bfloat16)
    other = gelu(pre_other[...].astype(jnp.float32)).astype(jnp.bfloat16)
    total[...] = dot(own, grad_own[...], (0, 0)) + dot(other, grad_other[...], (0, 0))
    size = keep.shape[2]
    for row in range(rows):
        start = pl.multiple_of(piece_at(info, 0, row, cores, rows) * size, size)
        keep[0, row] = total[pl.ds(start, size), :].astype(jnp.bfloat16)
        start = pl.multiple_of(piece_at(info, 1, row, cores, rows) * size, size)
        send[0, row] = total[pl.ds(start, size), :].astype(jnp.bfloat16)


def weight_partials(info, ids, pre, pre_other, grad, grad_other, block, rows):
    count = pre_other.shape[1] // block
    tokens, width = grad.shape
    size = block // (2 * rows)
    whole = pl.BlockSpec((tokens, width), lambda j, *_: (0, 0))
    out = jax.ShapeDtypeStruct((count, rows, size, width), jnp.bfloat16)
    out_spec = pl.BlockSpec((1, rows, size, width), lambda j, *_: (j, 0, 0, 0))
    return pl.pallas_call(
        functools.partial(weight_terms, 2, rows),
        out_shape=(out, out),
        grid_spec=pltpu.PrefetchScalarGridSpec(
            num_scalar_prefetch=2,
            grid=(count,),
            in_specs=[
                pl.BlockSpec((tokens, block), lambda j, info, ids: (0, ids[j])),
                pl.BlockSpec((tokens, block), lambda j, *_: (0, j)),
                whole,
                whole,
            ],
            out_specs=(out_spec, out_spec),
            scratch_shapes=[pltpu.VMEM((block, width), jnp.float32)],
        ),
        compiler_params=pltpu.CompilerParams(vmem_limit_bytes=VMEM_LIMIT),
        cost_estimate=pl.CostEstimate(
            flops=4 * tokens * block * count * width,
            bytes_accessed=4 * count * block * (tokens + width),
            transcendentals=2 * tokens * block * count,
        ),
        name="weight_partials",
    )(info, ids, pre, pre_other, grad, grad_other)


def token_terms(cores, rows, counts, first, info, ids, *refs):
    refs = list(refs)
    pre_own, pre_other, grad_own, grad_other = refs[:4]
    del refs[:4]
    pieces = []
    for count in counts:
        pieces.append(refs[:count])
        del refs[:count]
    if not first:
        total_in = refs[0]
        del refs[:2]
    grads_own, grads_other, total, grads, weights = refs
    tokens = pre_own.shape[0]
    step = pl.program_id(0)

    @pl.when(step == 0)
    def _():
        grads[:tokens] = grad_own[...]
        grads[tokens:] = grad_other[...]
        if first:
            total[...] = jnp.zeros_like(total)
        else:
            total[...] = total_in[...]

    for place, parts in enumerate(pieces):

        @pl.when(step == place)
        def _():
            if len(parts) == 1:
                weights[...] = parts[0][...]
            else:
                for number, part in enumerate(parts):
                    size = part.shape[0]
                    at = piece_at(info, number // rows, number % rows, cores, rows)
                    weights[pl.ds(pl.multiple_of(at * size, size), size), :] = part[...]

    own, own_slope = gelu_parts(pre_own[...].astype(jnp.float32))
    other, other_slope = gelu_parts(pre_other[...].astype(jnp.float32))
    matrix = weights[...]
    back = dot(grads[...], matrix, (1, 1))
    grads_own[...] = (back[:tokens] * own_slope).astype(jnp.bfloat16)
    grads_other[...] = (back[tokens:] * other_slope).astype(jnp.bfloat16)
    hidden = jnp.concatenate([own, other], axis=0).astype(jnp.bfloat16)
    total[...] += dot(hidden, matrix, (1, 0))


def token_partials(info, ids, pre, pre_other, grad, grad_other, pieces, rows, carried):
    count = len(pieces)
    block = pre_other.shape[1] // count
    tokens, width = grad.shape
    first = carried is None
    flat = [part for parts in pieces for part in parts]
    whole = pl.BlockSpec((tokens, width), lambda j, *_: (0, 0))
    total_spec = pl.BlockSpec((2 * tokens, width), lambda j, *_: (0, 0))
    in_specs = [
        pl.BlockSpec((tokens, block), lambda j, info, ids: (0, ids[j])),
        pl.BlockSpec((tokens, block), lambda j, *_: (0, j)),
        whole,
        whole,
        *[pl.BlockSpec(part.shape, lambda j, *_: (0, 0)) for part in flat],
    ]
    args = [info, ids, pre, pre_other, grad, grad_other, *flat]
    aliases = {}
    if not first:
        in_specs += [total_spec, pl.BlockSpec(memory_space=pl.ANY)]
        aliases = {len(args) + 1: 0}
        args += list(carried)
    return pl.pallas_call(
        functools.partial(token_terms, 2, rows, tuple(len(parts) for parts in pieces), first),
        out_shape=(
            jax.ShapeDtypeStruct(pre.shape, jnp.bfloat16),
            jax.ShapeDtypeStruct((tokens, block * count), jnp.bfloat16),
            jax.ShapeDtypeStruct((2 * tokens, width), jnp.float32),
        ),
        grid_spec=pltpu.PrefetchScalarGridSpec(
            num_scalar_prefetch=2,
            grid=(count,),
            in_specs=in_specs,
            out_specs=(
                pl.BlockSpec((tokens, block), lambda j, info, ids: (0, ids[j])),
                pl.BlockSpec((tokens, block), lambda j, *_: (0, j)),
                total_spec,
            ),
            scratch_shapes=[
                pltpu.VMEM((2 * tokens, width), jnp.bfloat16),
                pltpu.VMEM((block, width), jnp.bfloat16),
            ],
        ),
        input_output_aliases=aliases,
        compiler_params=pltpu.CompilerParams(vmem_limit_bytes=VMEM_LIMIT),
        cost_estimate=pl.CostEstimate(
            flops=8 * tokens * block * count * width,
            bytes_accessed=2 * count * block * (4 * tokens + width),
            transcendentals=2 * tokens * block * count,
        ),
        name="token_partials",
    )(*args)


def place_columns(ids, arrived, target):
    count = ids.shape[0]
    tokens = target.shape[0]
    block = arrived.shape[1] // count

    def copy(ids, arrived, target_in, target_out):
        target_out[...] = arrived[...]

    return pl.pallas_call(
        copy,
        out_shape=jax.ShapeDtypeStruct(target.shape, target.dtype),
        grid_spec=pltpu.PrefetchScalarGridSpec(
            num_scalar_prefetch=1,
            grid=(count,),
            in_specs=[
                pl.BlockSpec((tokens, block), lambda j, *_: (0, j)),
                pl.BlockSpec(memory_space=pl.ANY),
            ],
            out_specs=pl.BlockSpec((tokens, block), lambda j, ids: (0, ids[j])),
        ),
        input_output_aliases={2: 0},
        name="place_columns",
    )(ids, arrived, target)


def place_rows(info, parts, rows, scale):
    size, width = parts[0].shape

    def fill(info, *refs):
        out = refs[-1]
        for number, part in enumerate(refs[:-1]):
            at = piece_at(info, number // rows, number % rows, 2, rows)
            out[pl.ds(pl.multiple_of(at * size, size), size), :] = part[...].astype(jnp.float32) * scale

    return pl.pallas_call(
        fill,
        out_shape=jax.ShapeDtypeStruct((size * len(parts), width), jnp.float32),
        grid_spec=pltpu.PrefetchScalarGridSpec(
            num_scalar_prefetch=1,
            grid=(1,),
            in_specs=[pl.BlockSpec(part.shape, lambda j, *_: (0, 0)) for part in parts],
            out_specs=pl.BlockSpec((size * len(parts), width), lambda j, *_: (0, 0)),
        ),
        name="place_rows",
    )(info, *parts)


def natural_order(parts, info, rows):
    size, width = parts[0].shape
    cube = jnp.stack(parts).reshape(2, rows, size, width)
    for axis in range(2):
        length = cube.shape[axis]
        double = jnp.concatenate([cube, cube], axis=axis)
        cube = lax.dynamic_slice_in_dim(double, lax.rem(length - info[axis], length), length, axis)
    return cube.reshape(2 * rows * size, width)


def body(mesh_shape, pre_gelu, out_grad, down_weight):
    groups, cycle = mesh_shape
    rows, deep = groups // 2, cycle // 2
    block = down_weight.shape[0]
    size = block // groups
    f32, bf16 = jnp.float32, jnp.bfloat16

    def moved(array, row=0, core=0, far=0, near=0):
        pairs = []
        for dp in range(groups):
            for blk in range(cycle):
                to_dp = (dp // 2 + row) % rows * 2 + (dp + core) % 2
                to_blk = (blk // 2 + far) % deep * 2 + (blk + near) % 2
                pairs.append((dp * cycle + blk, to_dp * cycle + to_blk))
        return lax.ppermute(array, AXES, pairs)

    dp, blk = lax.axis_index("dp"), lax.axis_index("blk")
    far, near, row, core = blk // 2, blk % 2, dp // 2, dp % 2
    info = jnp.stack([core, row]).astype(jnp.int32)
    order = [*range(1, deep), 0]
    cut = (deep + 1) // 2
    halves = [order[:cut], order[cut:]]
    chunk_of = lambda j: lax.rem(far + j, deep) * 2
    own_ids = [jnp.stack([chunk_of(j) + near for j in half]).astype(jnp.int32) for half in halves]
    other_ids = [jnp.stack([chunk_of(j) + 1 - near for j in half]).astype(jnp.int32) for half in halves]

    grad_other = moved(out_grad, near=1)
    pre_others = []
    for half in halves:
        columns = [
            lax.dynamic_slice_in_dim(pre_gelu, (chunk_of(j) + 1 - near) * block, block, 1) for j in half
        ]
        pre_others.append(moved(jnp.concatenate(columns, axis=1), near=1))

    piece = lax.dynamic_slice_in_dim(down_weight, (core * rows + row) * size, size, 0)
    weights = {0: [down_weight]}
    for j in range(1, deep):
        mine = moved(piece, far=-j)
        parts = [mine] + [moved(mine, row=-i) for i in range(1, rows)]
        parts += [moved(part, core=1) for part in parts]
        weights[j] = parts if size % 16 == 0 else [natural_order(parts, info, rows)]

    summed = {}
    for half, ids, pre_other in zip(halves, own_ids, pre_others):
        keep, send = weight_partials(info, ids, pre_gelu, pre_other, out_grad, grad_other, block, rows)
        got = moved(send, core=1)
        both = keep.astype(f32) + got.astype(f32)
        total = both[:, 0]
        for i in range(1, rows):
            total = total + moved(both[:, i].astype(bf16), row=i).astype(f32)
        for place, j in enumerate(half):
            summed[j] = total[place]
    mine = summed[0]
    for j in range(1, deep):
        mine = mine + moved(summed[j].astype(bf16), far=j).astype(f32)
    mine = mine.astype(bf16)
    parts = [mine] + [moved(mine, row=-i) for i in range(1, rows)]
    parts += [moved(part, core=1) for part in parts]
    tokens_all = pre_gelu.shape[0] * groups * cycle
    weight_grad = place_rows(info, parts, rows, 1.0 / math.sqrt(tokens_all))

    carried, returned = None, []
    for half, ids, pre_other in zip(halves, own_ids, pre_others):
        pre_grad, grads_other, total = token_partials(
            info, ids, pre_gelu, pre_other, out_grad, grad_other, [weights[j] for j in half], rows, carried
        )
        carried = (total, pre_grad)
        returned.append(moved(grads_other, near=1))
    tokens = pre_gelu.shape[0]
    out_back = moved(total[tokens:].astype(bf16), near=1)
    block_out = (total[:tokens] + out_back.astype(f32)).astype(bf16)
    for ids, arrived in zip(other_ids, returned):
        pre_grad = place_columns(ids, arrived, pre_grad)
    return block_out, pre_grad, weight_grad


def solution(mesh):
    shape = (mesh.shape["dp"], mesh.shape["blk"])
    spread = P(("dp", "blk"), None)
    specs = (spread, spread, P("blk", None))
    return jax.shard_map(
        functools.partial(body, shape), mesh=mesh, in_specs=specs, out_specs=specs, check_vma=False
    )
```
